256 devices in a mesh: circ: 64 (over x_lo, y, z), span: 4 (over x_hi, core).
Axes of the slice: x: 4 (x_hi: 2, x_lo: 2; x = x_hi * 2 + x_lo), y: 4, z: 8, core: 2. Of those that a mesh axis runs over, the one named last changes fastest.
Arguments:
- coefficients: float32 [65, 5, 16, 4096], P(None, None, 'span', 'circ'), may hold values from -3 to 3
- local_step: float32 [16, 2048, 256], P('span', 'circ'), may hold values from 0.1 to 0.4
- jacobian: float32 [3, 5, 5], replicated, may hold values from -2.5 to 2.5
- harmonic_numbers: int32 [32], replicated, may hold values from 1 to 64
- nodal_diameter: int32 [1], replicated, may hold values from 1 to 64
Outputs:
- new_state: float32 [5, 16, 2048, 256], P(None, 'span', 'circ')
The draws below stay inside these ranges and needn't reach their ends.
All inputs are finite; a program needn't handle non-finite values.
Results may differ from the reference program's by a relative error of at most 0.0001.
Values sent between devices are 32-bit elements; how exact they have to be, the bound alone decides.
No kernel may reach another device: no remote copies, remote signals or barrier semaphores. Data moves between devices by JAX's collectives and lax.ppermute only.
A program may use at most 128 MiB of HBM per device.

```python
import math
import jax
import jax.numpy as jnp
from jax import lax

HARM = 32
VARS = 5
NCOEF = 65
PASS = 128
SPAN_CELLS = 16
PITCH = 16
AXIAL = 256


def set_ends(entries, own_key, low, high):
    longest = entries.shape.index(max(entries.shape))
    spots = []
    for shift in (0, 1):
        where = [jax.random.randint(jax.random.fold_in(own_key, axis), (), 0, length) for axis, length in enumerate(entries.shape)]
        where[longest] = (where[longest] + shift) % entries.shape[longest]
        spots.append(tuple(where))
    return entries.at[spots[0]].set(low).at[spots[1]].set(high)


def shard_levels(own_key, extent, shards, smallest, high):
    def one(axis_at, parts):
        draws = jax.random.uniform(jax.random.fold_in(jax.random.fold_in(own_key, 6), axis_at), (parts,), jnp.float32, smallest / len(shards), high / len(shards))
        return jnp.repeat(jnp.exp(draws), extent[axis_at] // parts).reshape((-1,) + (1,) * (len(extent) - axis_at - 1))

    factor_of = one(*shards[0])
    for cut in shards[1:]:
        factor_of = factor_of * one(*cut)
    return factor_of


def centred(own_key, extent, scale, reach, cuts=(), kind=jnp.bfloat16):
    values = scale * jax.random.normal(own_key, extent, jnp.float32)
    if cuts:
        values = values * shard_levels(own_key, extent, cuts, -0.22, 0.18)
    return jnp.clip(values, -reach, reach).astype(kind)


def setup_inputs(seed: int = 0) -> dict:
    arg_keys = jax.random.split(jax.random.key(seed), 6)
    return {
        "coefficients": centred(arg_keys[0], (NCOEF, VARS, SPAN_CELLS, PITCH * AXIAL), 0.2, 3.0, ((2, 4), (3, 64)), jnp.float32),
        "local_step": jnp.clip(jnp.exp(math.log(0.4) - 1.3862944 * jax.random.uniform(arg_keys[1], (SPAN_CELLS, PASS * PITCH, AXIAL), jnp.float32) ** shard_levels(arg_keys[1], (SPAN_CELLS, PASS * PITCH, AXIAL), ((0, 4), (1, 64)), -0.2, 0.2)), 0.1, 0.4),
        "jacobian": centred(arg_keys[2], (3, VARS, VARS), VARS ** -0.5, 2.5, (), jnp.float32),
        "harmonic_numbers": set_ends(jax.random.randint(arg_keys[3], (HARM,), 1, 2 * HARM + 1), jax.random.fold_in(arg_keys[3], 1), 1, 2 * HARM).astype(jnp.int32),
        "nodal_diameter": jax.random.randint(arg_keys[4], (1,), 1, PASS // 2 + 1).astype(jnp.int32),
    }


section_weight = 0.5
dissipation = 0.125


def phase_table(harmonic_numbers, nodal_diameter, passages, cycle_count):
    phase_turn = (harmonic_numbers[None, :] * nodal_diameter[0]) % cycle_count
    phase_turn = (phase_turn * passages[:, None]) % cycle_count
    phase_angle = phase_turn.astype(jnp.float32) * jnp.float32(2.0 * math.pi / cycle_count)
    mean_column = jnp.ones((passages.shape[0], 1), jnp.float32)
    return jnp.concatenate([mean_column, jnp.cos(phase_angle), jnp.sin(phase_angle)], axis=1)


def section_update(flow_state, span_pad, pitch_pad, jacobian, local_step):
    axial_pad = jnp.pad(flow_state, ((0, 0), (0, 0), (0, 0), (1, 1)))
    neighbours = [(span_pad[:, 2:], span_pad[:, :-2]),
                  (pitch_pad[:, :, 2:], pitch_pad[:, :, :-2]),
                  (axial_pad[:, :, :, 2:], axial_pad[:, :, :, :-2])]
    resid = jnp.zeros(flow_state.shape, jnp.float32)
    for direction in range(3):
        plus_side, minus_side = neighbours[direction]
        flux_part = jnp.einsum('vw,wsqa->vsqa', jacobian[direction], 0.5 * (plus_side - minus_side),
                               precision=lax.Precision.HIGHEST)
        resid = resid + flux_part - dissipation * (plus_side - 2.0 * flow_state + minus_side)
    return flow_state - section_weight * local_step[None] * resid


def reference(coefficients, local_step, jacobian, harmonic_numbers, nodal_diameter):
    passages = jnp.arange(PASS, dtype=jnp.int32)
    phases = phase_table(harmonic_numbers, nodal_diameter, passages, PASS)
    fields = jnp.einsum('pi,ivsc->pvsc', phases, coefficients, precision=lax.Precision.HIGHEST)
    fields = fields.reshape(PASS, VARS, SPAN_CELLS, PITCH, AXIAL)
    flow_state = fields.transpose(1, 2, 0, 3, 4).reshape(VARS, SPAN_CELLS, PASS * PITCH, AXIAL)
    span_pad = jnp.pad(flow_state, ((0, 0), (1, 1), (0, 0), (0, 0)))
    pitch_pad = jnp.concatenate([flow_state[:, :, -1:], flow_state, flow_state[:, :, :1]], axis=2)
    return section_update(flow_state, span_pad, pitch_pad, jacobian, local_step)
```

```python
import jax, jax.numpy as jnp
from jax import lax
from jax.sharding import PartitionSpec as P
import math

def phase_table(h, nd, passages, n):
    t = h[None, :] * nd[0] % n
    t = t * passages[:, None] % n
    ang = t.astype(jnp.float32) * jnp.float32(2.0 * math.pi / n)
    return jnp.concatenate([jnp.ones((passages.shape[0], 1), jnp.float32), jnp.cos(ang), jnp.sin(ang)], axis=1)

def extended(array, sides, width, wrap):
    for axis, dim in sides:
        count, length = (lax.axis_size(axis), array.shape[dim])
        up = [(i, (i + 1) % count) for i in range(count if wrap else count - 1)]
        down = [(j, i) for i, j in up]
        last = lax.slice_in_dim(array, length - width, length, axis=dim)
        initial = lax.slice_in_dim(array, 0, width, axis=dim)
        before = lax.ppermute(last, axis, up)
        after = lax.ppermute(initial, axis, down)
        array = jnp.concatenate([before, array, after], axis=dim)
    return array

def section_update(flow_state, span_pad, pitch_pad, jacobian, local_step):
    axial_pad = jnp.pad(flow_state, ((0, 0), (0, 0), (0, 0), (1, 1)))
    neighbours = [
        (span_pad[:, 2:], span_pad[:, :-2]),
        (pitch_pad[:, :, 2:], pitch_pad[:, :, :-2]),
        (axial_pad[:, :, :, 2:], axial_pad[:, :, :, :-2]),
    ]
    resid = jnp.zeros(flow_state.shape, jnp.float32)
    for direction in range(3):
        p, m = neighbours[direction]
        f = jnp.einsum("vw,wsqa->vsqa", jacobian[direction], 0.5 * (p - m), precision=lax.Precision.HIGHEST)
        resid = resid + f - 0.125 * (p - 2.0 * flow_state + m)
    return flow_state - 0.5 * local_step[None] * resid

def local(coefficients, local_step, jacobian, harmonic_numbers, nodal_diameter):
    phases = phase_table(harmonic_numbers, nodal_diameter, jnp.arange(128, dtype=jnp.int32), 128)
    f = jnp.einsum("pi,ivk->pvk", phases, coefficients.reshape(65, 5, 256), precision=lax.Precision.HIGHEST)
    f = f.reshape(64, 2, 5, 2, 128).transpose(0, 2, 1, 3, 4).reshape(64, 5, 4, 128)
    r = lax.all_to_all(f, "circ", 0, 0, tiled=True)
    r = r.reshape(16, 4, 5, 2, 2, 2, 64)
    flow = r.transpose(2, 4, 5, 3, 0, 1, 6).reshape(5, 4, 32, 256)
    pitch_pad = extended(flow, (("circ", 2),), 1, True)
    span_pad = extended(flow, (("span", 1),), 1, False)
    return section_update(flow, span_pad, pitch_pad, jacobian, local_step)

def solution(mesh):
    in_specs = (P(None, None, "span", "circ"), P("span", "circ", None), P(), P(), P())
    return jax.shard_map(local, mesh=mesh, in_specs=in_specs, out_specs=P(None, "span", "circ", None), check_vma=False)
```

```python
import functools
import math

import jax
import jax.numpy as jnp
from jax import lax
from jax.experimental import pallas as pl
from jax.experimental.pallas import tpu as pltpu
from jax.sharding import PartitionSpec as P

VMEM = pl.BlockSpec(memory_space=pltpu.VMEM)
SMEM = pl.BlockSpec(memory_space=pltpu.SMEM)
F32 = jnp.float32
ROWS = 20


def cos_turns(index):
    folded = jnp.where(index > 64, 128 - index, index)
    flip = folded > 32
    quarter = jnp.where(flip, 64 - folded, folded).astype(F32) * F32(math.pi / 64)
    square = quarter * quarter
    terms = [1.0, -1.0 / 2, 1.0 / 24, -1.0 / 720, 1.0 / 40320, -1.0 / 3628800, 1.0 / 479001600, -1.0 / 87178291200]
    value = jnp.full(index.shape, terms[-1], F32)
    for term in terms[-2::-1]:
        value = value * square + F32(term)
    return jnp.where(flip, -value, value)


def expand_kernel(coef_ref, harm_ref, nodal_ref, out_ref):
    harm = jnp.concatenate([harm_ref[...], jnp.zeros((1, 96), jnp.int32)], axis=1)
    lane = lax.broadcasted_iota(jnp.int32, (8, 128), 1)[:1]
    turns = (pltpu.roll(harm, 1, 1) + pltpu.roll(harm, 33, 1)) * nodal_ref[0] & 127
    row = lax.broadcasted_iota(jnp.int32, (128, 128), 0)
    passage = jnp.where(row < 64, 2 * row, 2 * row - 127)
    index = turns * passage & 127
    index = jnp.where(lane > 32, index + 96 & 127, index)
    phases = cos_turns(index)[:, :65]
    for pair in range(10):
        block = lax.dot_general(
            phases,
            coef_ref[pair * 128 : pair * 128 + 128, :],
            (((1,), (1,)), ((), ())),
            precision=lax.Precision.HIGHEST,
            preferred_element_type=F32,
        )
        out_ref[pl.ds(pair, 64, ROWS), :] = block[:64]
        out_ref[pl.ds(pair + 10, 64, ROWS), :] = block[64:]


def gather_kernel(got_ref, parity_ref, flow_ref, inner_ref, outer_ref, first_ref, final_ref):
    low = lax.broadcasted_iota(jnp.int32, (16, 128), 1) < 64
    even = parity_ref[0] == 0
    for p in range(2):
        for v in range(5):
            for h in range(2):
                row = p * 10 + v * 2 + h
                parts = [got_ref[pl.ds(a * ROWS + row, 16, 4 * ROWS), :] for a in range(4)]
                turned = [pltpu.roll(x, 64, 1) for x in parts]
                for b in range(2):
                    cols = slice(128 * b, 128 * b + 128)
                    base = (v * 4 + 2 * h) * 32 + p * 16
                    flow_ref[base : base + 16, cols] = jnp.where(low, parts[2 * b], turned[2 * b + 1])
                    flow_ref[base + 32 : base + 48, cols] = jnp.where(low, turned[2 * b], parts[2 * b + 1])
    for v in range(5):
        bottom = flow_ref[v * 128 : v * 128 + 32, :]
        top = flow_ref[v * 128 + 96 : v * 128 + 128, :]
        inner_ref[v * 32 : v * 32 + 32, :] = jnp.where(even, top, bottom)
        outer_ref[v * 32 : v * 32 + 32, :] = jnp.where(even, bottom, top)
    for i in range(20):
        first_ref[i : i + 1, :] = flow_ref[i * 32 : i * 32 + 1, :]
        final_ref[i : i + 1, :] = flow_ref[i * 32 + 31 : i * 32 + 32, :]


def section_kernel(flow_ref, inner_ref, outer_ref, before_ref, after_ref, step_ref, jac_ref, parity_ref, out_ref):
    even = parity_ref[0] == 0
    row = lax.broadcasted_iota(jnp.int32, (8, 256), 0)
    lane = lax.broadcasted_iota(jnp.int32, (8, 256), 1)
    at_top, at_bottom = row == 0, row == 7
    at_left, at_right = lane == 0, lane == 255
    half = [[[0.5 * jac_ref[d, v, w] for w in range(5)] for v in range(5)] for d in range(3)]
    for s in range(4):
        for t in range(4):
            diffs, smooth = [], []
            for v in range(5):
                base = (v * 4 + s) * 32 + t * 8
                here = flow_ref[base : base + 8, :]
                side = slice(v * 32 + t * 8, v * 32 + t * 8 + 8)
                if s == 0:
                    s_minus = jnp.where(even, outer_ref[side, :], inner_ref[side, :])
                else:
                    s_minus = flow_ref[base - 32 : base - 24, :]
                if s == 3:
                    s_plus = jnp.where(even, inner_ref[side, :], outer_ref[side, :])
                else:
                    s_plus = flow_ref[base + 32 : base + 40, :]
                above = flow_ref[base - 1 : base, :] if t else before_ref[v * 4 + s : v * 4 + s + 1, :]
                below = flow_ref[base + 8 : base + 9, :] if t < 3 else after_ref[v * 4 + s : v * 4 + s + 1, :]
                p_minus = jnp.where(at_top, above, pltpu.roll(here, 1, 0))
                p_plus = jnp.where(at_bottom, below, pltpu.roll(here, 7, 0))
                a_minus = jnp.where(at_left, 0.0, pltpu.roll(here, 1, 1))
                a_plus = jnp.where(at_right, 0.0, pltpu.roll(here, 255, 1))
                diffs.append((s_plus - s_minus, p_plus - p_minus, a_plus - a_minus))
                total = (s_plus + s_minus) + (p_plus + p_minus) + (a_plus + a_minus)
                smooth.append((here, 0.75 * here - 0.125 * total))
            scale = 0.5 * step_ref[s * 32 + t * 8 : s * 32 + t * 8 + 8, :]
            for v in range(5):
                here, resid = smooth[v]
                for d in range(3):
                    for w in range(5):
                        resid = resid + half[d][v][w] * diffs[w][d]
                base = (v * 4 + s) * 32 + t * 8
                out_ref[base : base + 8, :] = here - scale * resid


def local(coefficients, local_step, jacobian, harmonic_numbers, nodal_diameter):
    shape = jax.ShapeDtypeStruct
    ring = lax.axis_size("circ")
    parity = (lax.axis_index("span") % 2).astype(jnp.int32).reshape(1)
    cells = coefficients.transpose(1, 2, 3, 0).reshape(1280, 65)
    sent = pl.pallas_call(
        expand_kernel,
        out_shape=shape((64 * ROWS, 128), F32),
        in_specs=[VMEM, VMEM, SMEM],
        out_specs=VMEM,
        name="expand",
        compiler_params=pltpu.CompilerParams(vmem_limit_bytes=8 << 20),
    )(cells, harmonic_numbers.reshape(1, 32), nodal_diameter)
    got = lax.all_to_all(sent.reshape(64, 5, 4, 128), "circ", 0, 0, tiled=True).reshape(64 * ROWS, 128)
    flow, inner, outer, first, final = pl.pallas_call(
        gather_kernel,
        out_shape=[shape((640, 256), F32), shape((160, 256), F32), shape((160, 256), F32), shape((20, 256), F32), shape((20, 256), F32)],
        in_specs=[VMEM, SMEM],
        out_specs=[VMEM] * 5,
        name="gather",
        compiler_params=pltpu.CompilerParams(vmem_limit_bytes=8 << 20),
    )(got, parity)
    outer = lax.ppermute(outer, "span", [(1, 2), (2, 1)])
    before = lax.ppermute(final, "circ", [(i, (i + 1) % ring) for i in range(ring)])
    after = lax.ppermute(first, "circ", [((i + 1) % ring, i) for i in range(ring)])
    inner = lax.ppermute(inner, "span", [(0, 1), (1, 0), (2, 3), (3, 2)])
    new = pl.pallas_call(
        section_kernel,
        out_shape=shape((640, 256), F32),
        in_specs=[VMEM] * 6 + [SMEM] * 2,
        out_specs=VMEM,
        name="section",
        compiler_params=pltpu.CompilerParams(vmem_limit_bytes=8 << 20),
    )(flow, inner, outer, before, after, local_step.reshape(128, 256), jacobian, parity)
    return new.reshape(5, 4, 32, 256)


def solution(mesh):
    in_specs = (P(None, None, "span", "circ"), P("span", "circ", None), P(), P(), P())
    out_specs = P(None, "span", "circ", None)
    return jax.shard_map(local, mesh=mesh, in_specs=in_specs, out_specs=out_specs, check_vma=False)
```

```python
import functools
import math

import jax
import jax.numpy as jnp
from jax import lax
from jax.experimental import pallas as pl
from jax.experimental.pallas import tpu as pltpu
from jax.sharding import PartitionSpec as P

VMEM = pl.BlockSpec(memory_space=pltpu.VMEM)
SMEM = pl.BlockSpec(memory_space=pltpu.SMEM)
F32 = jnp.float32
HBM = pl.BlockSpec(memory_space=pltpu.HBM)
ROWS = 20


def cos_turns(index):
    folded = jnp.where(index > 64, 128 - index, index)
    flip = folded > 32
    quarter = jnp.where(flip, 64 - folded, folded).astype(F32) * F32(math.pi / 64)
    square = quarter * quarter
    terms = [1.0, -1.0 / 2, 1.0 / 24, -1.0 / 720, 1.0 / 40320, -1.0 / 3628800, 1.0 / 479001600, -1.0 / 87178291200]
    value = jnp.full(index.shape, terms[-1], F32)
    for term in terms[-2::-1]:
        value = value * square + F32(term)
    return jnp.where(flip, -value, value)


def expand_kernel(coef_hbm, harm_hbm, nodal_hbm, out_ref, coef_ref, harm_ref, nodal_ref, sems):
    loads = [
        pltpu.make_async_copy(harm_hbm, harm_ref, sems.at[0]),
        pltpu.make_async_copy(nodal_hbm, nodal_ref, sems.at[1]),
        pltpu.make_async_copy(coef_hbm, coef_ref, sems.at[2]),
    ]
    for load in loads:
        load.start()
    lane = lax.broadcasted_iota(jnp.int32, (128, 128), 1)
    row = lax.broadcasted_iota(jnp.int32, (128, 128), 0)
    passage = jnp.where(row < 64, 2 * row, 2 * row - 127)
    loads[0].wait()
    loads[1].wait()
    harm = jnp.concatenate([harm_ref[...], jnp.zeros((1, 96), jnp.int32)], axis=1)
    turns = (pltpu.roll(harm, 1, 1) + pltpu.roll(harm, 33, 1)) * nodal_ref[...] & 127
    index = turns * passage & 127
    index = jnp.where(lane > 32, index + 96 & 127, index)
    phases = cos_turns(index)[:, :65]
    wide = phases.astype(jnp.bfloat16)
    rest = (phases - wide.astype(F32)).astype(jnp.bfloat16)
    product = functools.partial(
        lax.dot_general, dimension_numbers=(((1,), (1,)), ((), ())), preferred_element_type=F32
    )
    loads[2].wait()
    for group in range(5):
        values = coef_ref[group * 256 : group * 256 + 256, :]
        high = values.astype(jnp.bfloat16)
        low = (values - high.astype(F32)).astype(jnp.bfloat16)
        block = product(wide, high) + (product(wide, low) + product(rest, high))
        for h in range(2):
            pair = group * 2 + h
            cols = slice(128 * h, 128 * h + 128)
            out_ref[pl.ds(pair, 64, ROWS), :] = block[:64, cols]
            out_ref[pl.ds(pair + 10, 64, ROWS), :] = block[64:, cols]


def gather_kernel(got_ref, parity_ref, flow_ref, inner_ref, outer_ref, near_ref, far_ref):
    low = lax.broadcasted_iota(jnp.int32, (16, 128), 1) < 64
    even = parity_ref[0] == 0
    circ_even = parity_ref[1] == 0
    for p in range(2):
        for v in range(5):
            for h in range(2):
                row = p * 10 + v * 2 + h
                parts = [got_ref[pl.ds(a * ROWS + row, 16, 4 * ROWS), :] for a in range(4)]
                turned = [pltpu.roll(x, 64, 1) for x in parts]
                for b in range(2):
                    cols = slice(128 * b, 128 * b + 128)
                    base = (v * 4 + 2 * h) * 32 + p * 16
                    flow_ref[base : base + 16, cols] = jnp.where(low, parts[2 * b], turned[2 * b + 1])
                    flow_ref[base + 32 : base + 48, cols] = jnp.where(low, turned[2 * b], parts[2 * b + 1])
    for v in range(5):
        bottom = flow_ref[v * 128 : v * 128 + 32, :]
        top = flow_ref[v * 128 + 96 : v * 128 + 128, :]
        inner_ref[v * 32 : v * 32 + 32, :] = jnp.where(even, top, bottom)
        outer_ref[v * 32 : v * 32 + 32, :] = jnp.where(even, bottom, top)
    for i in range(20):
        first = flow_ref[i * 32 : i * 32 + 1, :]
        final = flow_ref[i * 32 + 31 : i * 32 + 32, :]
        near_ref[i : i + 1, :] = jnp.where(circ_even, final, first)
        far_ref[i : i + 1, :] = jnp.where(circ_even, first, final)


def halves(jac_ref, d):
    return [[0.5 * jac_ref[d, v, w] for w in range(5)] for v in range(5)]


def section_kernel(flow_ref, step_ref, jac_ref, part_ref):
    row = lax.broadcasted_iota(jnp.int32, (8, 256), 0)
    lane = lax.broadcasted_iota(jnp.int32, (8, 256), 1)
    at_top, at_bottom = row == 0, row == 7
    at_left, at_right = lane == 0, lane == 255
    half = [halves(jac_ref, d) for d in range(3)]
    for s in range(4):
        for t in range(4):
            diffs, smooth = [], []
            for v in range(5):
                base = (v * 4 + s) * 32 + t * 8
                here = flow_ref[base : base + 8, :]
                s_minus = flow_ref[base - 32 : base - 24, :] if s else jnp.zeros_like(here)
                s_plus = flow_ref[base + 32 : base + 40, :] if s < 3 else jnp.zeros_like(here)
                above = flow_ref[base - 1 : base, :] if t else 0.0
                below = flow_ref[base + 8 : base + 9, :] if t < 3 else 0.0
                p_minus = jnp.where(at_top, above, pltpu.roll(here, 1, 0))
                p_plus = jnp.where(at_bottom, below, pltpu.roll(here, 7, 0))
                a_minus = jnp.where(at_left, 0.0, pltpu.roll(here, 1, 1))
                a_plus = jnp.where(at_right, 0.0, pltpu.roll(here, 255, 1))
                diffs.append((s_plus - s_minus, p_plus - p_minus, a_plus - a_minus))
                total = (s_plus + s_minus) + (p_plus + p_minus) + (a_plus + a_minus)
                smooth.append((here, 0.75 * here - 0.125 * total))
            scale = 0.5 * step_ref[s * 32 + t * 8 : s * 32 + t * 8 + 8, :]
            for v in range(5):
                here, resid = smooth[v]
                for d in range(3):
                    for w in range(5):
                        resid = resid + half[d][v][w] * diffs[w][d]
                base = (v * 4 + s) * 32 + t * 8
                part_ref[base : base + 8, :] = here - scale * resid


def applied(half, sign, rows):
    out = []
    for v in range(5):
        total = -0.125 * rows[v]
        for w in range(5):
            total = total + (sign * half[v][w]) * rows[w]
        out.append(total)
    return out


def finish_kernel(part_ref, far_ref, outer_ref, near_ref, inner_ref, step_ref, jac_ref, parity_ref, out_ref):
    even = parity_ref[0] == 0
    circ_even = parity_ref[1] == 0
    half = halves(jac_ref, 0)
    for s in (0, 3):
        for t in range(4):
            rows = []
            for v in range(5):
                side = slice(v * 32 + t * 8, v * 32 + t * 8 + 8)
                inner, outer = inner_ref[side, :], outer_ref[side, :]
                rows.append(jnp.where(even, outer, inner) if s == 0 else jnp.where(even, inner, outer))
            scale = 0.5 * step_ref[s * 32 + t * 8 : s * 32 + t * 8 + 8, :]
            terms = applied(half, 1.0 if s else -1.0, rows)
            for v in range(5):
                base = (v * 4 + s) * 32 + t * 8
                out_ref[base : base + 8, :] = part_ref[base : base + 8, :] - scale * terms[v]
    for v in range(5):
        base = v * 128 + 32
        out_ref[base : base + 64, :] = part_ref[base : base + 64, :]
    half = halves(jac_ref, 1)
    for edge, sign in ((0, -1.0), (31, 1.0)):
        rows = []
        for v in range(5):
            near, far = near_ref[v * 4 : v * 4 + 4, :], far_ref[v * 4 : v * 4 + 4, :]
            rows.append(jnp.where(circ_even, near, far) if edge else jnp.where(circ_even, far, near))
        terms = applied(half, sign, rows)
        for s in range(4):
            scale = 0.5 * step_ref[s * 32 + edge : s * 32 + edge + 1, :]
            for v in range(5):
                at = (v * 4 + s) * 32 + edge
                out_ref[at : at + 1, :] = out_ref[at : at + 1, :] - scale * terms[v][s : s + 1, :]


def local(coefficients, local_step, jacobian, harmonic_numbers, nodal_diameter):
    shape = jax.ShapeDtypeStruct
    ring = lax.axis_size("circ")
    parity = jnp.stack([lax.axis_index("span") & 1, lax.axis_index("circ") & 1]).astype(jnp.int32)
    cells = coefficients.transpose(1, 2, 3, 0).reshape(1280, 65)
    params = pltpu.CompilerParams(vmem_limit_bytes=8 << 20)
    sent = pl.pallas_call(
        expand_kernel,
        out_shape=shape((64 * ROWS, 128), F32),
        in_specs=[HBM, HBM, HBM],
        out_specs=VMEM,
        scratch_shapes=[
            pltpu.VMEM((1280, 65), F32),
            pltpu.VMEM((1, 32), jnp.int32),
            pltpu.VMEM((1, 1), jnp.int32),
            pltpu.SemaphoreType.DMA((3,)),
        ],
        name="expand",
    )(cells, harmonic_numbers.reshape(1, 32), nodal_diameter.reshape(1, 1))
    got = lax.all_to_all(sent.reshape(64, 5, 4, 128), "circ", 0, 0, tiled=True).reshape(64 * ROWS, 128)
    sizes = [(640, 256), (160, 256), (160, 256), (20, 256), (20, 256)]
    flow, inner, outer, near, far = pl.pallas_call(
        gather_kernel,
        out_shape=[shape(size, F32) for size in sizes],
        in_specs=[VMEM, SMEM],
        out_specs=[VMEM] * 5,
        name="gather",
        compiler_params=params,
    )(got, parity)
    pairs = [(i, i + 1) for i in range(0, ring, 2)]
    between = [(i, (i + 1) % ring) for i in range(1, ring, 2)]
    far = lax.ppermute(far, "circ", between + [(j, i) for i, j in between])
    outer = lax.ppermute(outer, "span", [(1, 2), (2, 1)])
    near = lax.ppermute(near, "circ", pairs + [(j, i) for i, j in pairs])
    inner = lax.ppermute(inner, "span", [(0, 1), (1, 0), (2, 3), (3, 2)])
    step = local_step.reshape(128, 256)
    part = pl.pallas_call(
        section_kernel,
        out_shape=shape((640, 256), F32),
        in_specs=[VMEM, VMEM, SMEM],
        out_specs=VMEM,
        name="section",
        compiler_params=params,
        cost_estimate=pl.CostEstimate(flops=20_000_000, bytes_accessed=1_500_000, transcendentals=0),
    )(flow, step, jacobian)
    new = pl.pallas_call(
        finish_kernel,
        out_shape=shape((640, 256), F32),
        in_specs=[VMEM] * 6 + [SMEM] * 2,
        out_specs=VMEM,
        name="finish",
        compiler_params=params,
    )(part, far, outer, near, inner, step, jacobian, parity)
    return new.reshape(5, 4, 32, 256)


def solution(mesh):
    in_specs = (P(None, None, "span", "circ"), P("span", "circ", None), P(), P(), P())
    out_specs = P(None, "span", "circ", None)
    return jax.shard_map(local, mesh=mesh, in_specs=in_specs, out_specs=out_specs, check_vma=False)
```

```python
import functools
import math

import jax
import jax.numpy as jnp
from jax import lax
from jax.experimental import pallas as pl
from jax.experimental.pallas import tpu as pltpu
from jax.sharding import PartitionSpec as P

VMEM = pl.BlockSpec(memory_space=pltpu.VMEM)
SMEM = pl.BlockSpec(memory_space=pltpu.SMEM)
F32 = jnp.float32
HBM = pl.BlockSpec(memory_space=pltpu.HBM)
ROWS = 20


def cos_turns(index):
    folded = jnp.where(index > 64, 128 - index, index)
    flip = folded > 32
    quarter = jnp.where(flip, 64 - folded, folded).astype(F32) * F32(math.pi / 64)
    square = quarter * quarter
    terms = [1.0, -1.0 / 2, 1.0 / 24, -1.0 / 720, 1.0 / 40320, -1.0 / 3628800, 1.0 / 479001600, -1.0 / 87178291200]
    value = jnp.full(index.shape, terms[-1], F32)
    for term in terms[-2::-1]:
        value = value * square + F32(term)
    return jnp.where(flip, -value, value)


def expand_kernel(coef_hbm, harm_hbm, nodal_hbm, out_ref, coef_ref, harm_ref, nodal_ref, sems):
    loads = [
        pltpu.make_async_copy(harm_hbm, harm_ref, sems.at[0]),
        pltpu.make_async_copy(nodal_hbm, nodal_ref, sems.at[1]),
        pltpu.make_async_copy(coef_hbm, coef_ref, sems.at[2]),
    ]
    for load in loads:
        load.start()
    lane = lax.broadcasted_iota(jnp.int32, (128, 128), 1)
    row = lax.broadcasted_iota(jnp.int32, (128, 128), 0)
    passage = jnp.where(row < 64, 2 * row, 2 * row - 127)
    loads[0].wait()
    loads[1].wait()
    harm = jnp.concatenate([harm_ref[...], jnp.zeros((1, 96), jnp.int32)], axis=1)
    turns = (pltpu.roll(harm, 1, 1) + pltpu.roll(harm, 33, 1)) * nodal_ref[0] & 127
    index = turns * passage & 127
    index = jnp.where(lane > 32, index + 96 & 127, index)
    phases = cos_turns(index)[:, :65]
    wide = phases.astype(jnp.bfloat16)
    rest = (phases - wide.astype(F32)).astype(jnp.bfloat16)
    product = functools.partial(
        lax.dot_general, dimension_numbers=(((1,), (1,)), ((), ())), preferred_element_type=F32
    )
    loads[2].wait()
    for group in range(5):
        values = coef_ref[group * 256 : group * 256 + 256, :]
        high = values.astype(jnp.bfloat16)
        low = (values - high.astype(F32)).astype(jnp.bfloat16)
        block = product(wide, high) + (product(wide, low) + product(rest, high))
        for h in range(2):
            pair = group * 2 + h
            cols = slice(128 * h, 128 * h + 128)
            out_ref[pl.ds(pair, 64, ROWS), :] = block[:64, cols]
            out_ref[pl.ds(pair + 10, 64, ROWS), :] = block[64:, cols]


def gather_kernel(got_ref, parity_ref, flow_ref, inner_ref, outer_ref, near_ref, far_ref):
    low = lax.broadcasted_iota(jnp.int32, (16, 128), 1) < 64
    for p in range(2):
        for v in range(5):
            for h in range(2):
                row = p * 10 + v * 2 + h
                parts = [got_ref[pl.ds(a * ROWS + row, 16, 4 * ROWS), :] for a in range(4)]
                turned = [pltpu.roll(x, 64, 1) for x in parts]
                for b in range(2):
                    cols = slice(128 * b, 128 * b + 128)
                    base = (v * 4 + 2 * h) * 32 + p * 16
                    flow_ref[base : base + 16, cols] = jnp.where(low, parts[2 * b], turned[2 * b + 1])
                    flow_ref[base + 32 : base + 48, cols] = jnp.where(low, turned[2 * b], parts[2 * b + 1])
    layer, row = parity_ref[0] * 96, parity_ref[1] * 31
    for v in range(5):
        inner_at = pl.multiple_of(v * 128 + 96 - layer, 32)
        outer_at = pl.multiple_of(v * 128 + layer, 32)
        inner_ref[v * 32 : v * 32 + 32, :] = flow_ref[pl.ds(inner_at, 32), :]
        outer_ref[v * 32 : v * 32 + 32, :] = flow_ref[pl.ds(outer_at, 32), :]
    for i in range(20):
        near_ref[i : i + 1, :] = flow_ref[pl.ds(i * 32 + 31 - row, 1), :]
        far_ref[i : i + 1, :] = flow_ref[pl.ds(i * 32 + row, 1), :]


def halves(jac_ref, d):
    return [[0.5 * jac_ref[d, v, w] for w in range(5)] for v in range(5)]


def section_kernel(flow_ref, step_ref, jac_ref, part_ref):
    row = lax.broadcasted_iota(jnp.int32, (8, 256), 0)
    lane = lax.broadcasted_iota(jnp.int32, (8, 256), 1)
    at_top, at_bottom = row == 0, row == 7
    at_left, at_right = lane == 0, lane == 255
    half = [halves(jac_ref, d) for d in range(3)]
    for s in range(4):
        for t in range(4):
            diffs, smooth = [], []
            for v in range(5):
                base = (v * 4 + s) * 32 + t * 8
                here = flow_ref[base : base + 8, :]
                s_minus = flow_ref[base - 32 : base - 24, :] if s else jnp.zeros_like(here)
                s_plus = flow_ref[base + 32 : base + 40, :] if s < 3 else jnp.zeros_like(here)
                above = flow_ref[base - 1 : base, :] if t else 0.0
                below = flow_ref[base + 8 : base + 9, :] if t < 3 else 0.0
                p_minus = jnp.where(at_top, above, pltpu.roll(here, 1, 0))
                p_plus = jnp.where(at_bottom, below, pltpu.roll(here, 7, 0))
                a_minus = jnp.where(at_left, 0.0, pltpu.roll(here, 1, 1))
                a_plus = jnp.where(at_right, 0.0, pltpu.roll(here, 255, 1))
                diffs.append((s_plus - s_minus, p_plus - p_minus, a_plus - a_minus))
                total = (s_plus + s_minus) + (p_plus + p_minus) + (a_plus + a_minus)
                smooth.append((here, 0.75 * here - 0.125 * total))
            scale = 0.5 * step_ref[s * 32 + t * 8 : s * 32 + t * 8 + 8, :]
            for v in range(5):
                here, resid = smooth[v]
                for d in range(3):
                    for w in range(5):
                        resid = resid + half[d][v][w] * diffs[w][d]
                base = (v * 4 + s) * 32 + t * 8
                part_ref[base : base + 8, :] = here - scale * resid


def applied(half, rows):
    out = []
    for v in range(5):
        total = -0.125 * rows[v]
        for w in range(5):
            total = total + half[v][w] * rows[w]
        out.append(total)
    return out


def finish_kernel(part_ref, far_ref, outer_ref, near_ref, inner_ref, step_ref, jac_ref, parity_ref, out_hbm, new_ref, sem):
    layer, row = parity_ref[0], parity_ref[1]
    half = halves(jac_ref, 1)
    for v in range(5):
        new_ref[v * 128 : v * 128 + 128, :] = part_ref[v * 128 : v * 128 + 128, :]
    for edge_ref, edge in ((near_ref, 1 - row), (far_ref, row)):
        sign = 2.0 * edge.astype(F32) - 1.0
        terms = applied([[sign * x for x in line] for line in half], [edge_ref[v * 4 : v * 4 + 4, :] for v in range(5)])
        for s in range(4):
            scale = 0.5 * step_ref[pl.ds(s * 32 + 31 * edge, 1), :]
            for v in range(5):
                at = pl.ds((v * 4 + s) * 32 + 31 * edge, 1)
                new_ref[at, :] = part_ref[at, :] - scale * terms[v][s : s + 1, :]
    copies = []
    for v in range(5):
        rows = slice(v * 128 + 32, v * 128 + 96)
        copies.append(pltpu.make_async_copy(new_ref.at[rows, :], out_hbm.at[rows, :], sem.at[v]))
        copies[-1].start()
    half = halves(jac_ref, 0)
    for i, (side_ref, side) in enumerate(((inner_ref, 1 - layer), (outer_ref, layer))):
        sign = 2.0 * side.astype(F32) - 1.0
        signed = [[sign * x for x in line] for line in half]
        for t in range(4):
            terms = applied(signed, [side_ref[v * 32 + t * 8 : v * 32 + t * 8 + 8, :] for v in range(5)])
            scale = 0.5 * step_ref[pl.ds(pl.multiple_of(side * 96 + t * 8, 8), 8), :]
            for v in range(5):
                at = pl.ds(pl.multiple_of(v * 128 + side * 96 + t * 8, 8), 8)
                new_ref[at, :] = new_ref[at, :] - scale * terms[v]
        for v in range(5):
            rows = pl.ds(pl.multiple_of(v * 128 + side * 96, 32), 32)
            copies.append(pltpu.make_async_copy(new_ref.at[rows, :], out_hbm.at[rows, :], sem.at[5 + 5 * i + v]))
            copies[-1].start()
    for copy in copies:
        copy.wait()


def local(coefficients, local_step, jacobian, harmonic_numbers, nodal_diameter):
    shape = jax.ShapeDtypeStruct
    ring = lax.axis_size("circ")
    parity = jnp.stack([lax.axis_index("span") & 1, lax.axis_index("circ") & 1]).astype(jnp.int32)
    cells = coefficients.transpose(1, 2, 3, 0).reshape(1280, 65)
    params = pltpu.CompilerParams(vmem_limit_bytes=8 << 20)
    sent = pl.pallas_call(
        expand_kernel,
        out_shape=shape((64 * ROWS, 128), F32),
        in_specs=[HBM, HBM, HBM],
        out_specs=VMEM,
        scratch_shapes=[
            pltpu.VMEM((1280, 65), F32),
            pltpu.VMEM((1, 32), jnp.int32),
            pltpu.SMEM((1,), jnp.int32),
            pltpu.SemaphoreType.DMA((3,)),
        ],
        name="expand",
    )(cells, harmonic_numbers.reshape(1, 32), nodal_diameter)
    got = lax.all_to_all(sent.reshape(64, 5, 4, 128), "circ", 0, 0, tiled=True).reshape(64 * ROWS, 128)
    sizes = [(640, 256), (160, 256), (160, 256), (20, 256), (20, 256)]
    flow, inner, outer, near, far = pl.pallas_call(
        gather_kernel,
        out_shape=[shape(size, F32) for size in sizes],
        in_specs=[VMEM, SMEM],
        out_specs=[VMEM] * 5,
        name="gather",
        compiler_params=params,
    )(got, parity)
    pairs = [(i, i + 1) for i in range(0, ring, 2)]
    between = [(i, (i + 1) % ring) for i in range(1, ring, 2)]
    far = lax.ppermute(far, "circ", between + [(j, i) for i, j in between])
    outer = lax.ppermute(outer, "span", [(1, 2), (2, 1)])
    near = lax.ppermute(near, "circ", pairs + [(j, i) for i, j in pairs])
    inner = lax.ppermute(inner, "span", [(0, 1), (1, 0), (2, 3), (3, 2)])
    step = local_step.reshape(128, 256)
    part = pl.pallas_call(
        section_kernel,
        out_shape=shape((640, 256), F32),
        in_specs=[VMEM, VMEM, SMEM],
        out_specs=VMEM,
        name="section",
        compiler_params=params,
        cost_estimate=pl.CostEstimate(flops=20_000_000, bytes_accessed=1_500_000, transcendentals=0),
    )(flow, step, jacobian)
    new = pl.pallas_call(
        finish_kernel,
        out_shape=shape((640, 256), F32),
        in_specs=[VMEM] * 6 + [SMEM] * 2,
        out_specs=HBM,
        scratch_shapes=[pltpu.VMEM((640, 256), F32), pltpu.SemaphoreType.DMA((15,))],
        name="finish",
        compiler_params=params,
    )(part, far, outer, near, inner, step, jacobian, parity)
    return new.reshape(5, 4, 32, 256)


def solution(mesh):
    in_specs = (P(None, None, "span", "circ"), P("span", "circ", None), P(), P(), P())
    out_specs = P(None, "span", "circ", None)
    return jax.shard_map(local, mesh=mesh, in_specs=in_specs, out_specs=out_specs, check_vma=False)
```

```python
import functools
import math

import jax
import jax.numpy as jnp
from jax import lax
from jax.experimental import pallas as pl
from jax.experimental.pallas import tpu as pltpu
from jax.sharding import PartitionSpec as P

VMEM = pl.BlockSpec(memory_space=pltpu.VMEM)
SMEM = pl.BlockSpec(memory_space=pltpu.SMEM)
HBM = pl.BlockSpec(memory_space=pltpu.HBM)
F32 = jnp.float32
ROWS = 20
LAYERS = ((0, 3), (1, 2))


def cos_turns(index):
    folded = jnp.where(index > 64, 128 - index, index)
    flip = folded > 32
    quarter = jnp.where(flip, 64 - folded, folded).astype(F32) * F32(math.pi / 64)
    square = quarter * quarter
    terms = [1.0, -1.0 / 2, 1.0 / 24, -1.0 / 720, 1.0 / 40320, -1.0 / 3628800, 1.0 / 479001600, -1.0 / 87178291200]
    value = jnp.full(index.shape, terms[-1], F32)
    for term in terms[-2::-1]:
        value = value * square + F32(term)
    return jnp.where(flip, -value, value)


def expand_kernel(coef_hbm, harm_hbm, nodal_ref, out_ref, coef_ref, harm_ref, sems):
    loads = [
        pltpu.make_async_copy(harm_hbm, harm_ref, sems.at[0]),
        pltpu.make_async_copy(coef_hbm, coef_ref, sems.at[1]),
    ]
    for load in loads:
        load.start()
    lane = lax.broadcasted_iota(jnp.int32, (128, 128), 1)
    row = lax.broadcasted_iota(jnp.int32, (128, 128), 0)
    passage = jnp.where(row < 64, 2 * row, 2 * row - 127)
    loads[0].wait()
    harm = jnp.concatenate([harm_ref[...], jnp.zeros((1, 96), jnp.int32)], axis=1)
    turns = (pltpu.roll(harm, 1, 1) + pltpu.roll(harm, 33, 1)) * nodal_ref[0] & 127
    index = turns * passage & 127
    index = jnp.where(lane > 32, index + 96 & 127, index)
    phases = cos_turns(index)[:, :65]
    wide = phases.astype(jnp.bfloat16)
    rest = (phases - wide.astype(F32)).astype(jnp.bfloat16)
    product = functools.partial(
        lax.dot_general, dimension_numbers=(((1,), (1,)), ((), ())), preferred_element_type=F32
    )
    loads[1].wait()
    for v in range(5):
        values = jnp.concatenate([coef_ref[pl.ds((v * 4 + s) * 64, 64), :] for s in (0, 3, 1, 2)], axis=0)
        high = values.astype(jnp.bfloat16)
        low = (values - high.astype(F32)).astype(jnp.bfloat16)
        block = product(wide, high) + (product(wide, low) + product(rest, high))
        for p in range(2):
            for m in range(2):
                out_ref[pl.ds(p * 10 + m * 5 + v, 64, ROWS), :] = block[p * 64 : p * 64 + 64, m * 128 : m * 128 + 128]


def paired(parts):
    low = lax.broadcasted_iota(jnp.int32, parts[0].shape, 1) < 64
    turned = [pltpu.roll(x, 64, 1) for x in parts]
    lower = [jnp.where(low, parts[2 * b], turned[2 * b + 1]) for b in range(2)]
    upper = [jnp.where(low, turned[2 * b], parts[2 * b + 1]) for b in range(2)]
    return lower, upper


def edges_kernel(got_ref, far_ref, outer_ref, near_ref, inner_ref, first_ref, final_ref):
    even, circ_even = (lax.axis_index(axis) & 1 == 0 for axis in ("span", "circ"))
    for rim_ref, source, passage in ((first_ref, 0, 0), (final_ref, 60, 1)):
        for m in range(2):
            start = passage * 10 + m * 5
            both = paired([got_ref[pl.ds((source + a) * ROWS + start, 5), :] for a in range(4)])
            for s, halves_of in zip(LAYERS[m], both):
                for b in range(2):
                    rim_ref[pl.ds(b * 20 + s, 5, 4), :] = halves_of[b]
    first, final = first_ref[...], final_ref[...]
    near_ref[...] = jnp.where(circ_even, final, first)
    far_ref[...] = jnp.where(circ_even, first, final)
    for p in range(2):
        for v in range(5):
            bottom, top = paired([got_ref[pl.ds(a * ROWS + p * 10 + v, 16, 4 * ROWS), :] for a in range(4)])
            rows = slice(v * 32 + p * 16, v * 32 + p * 16 + 16)
            for b in range(2):
                cols = slice(128 * b, 128 * b + 128)
                inner_ref[rows, cols] = jnp.where(even, top[b], bottom[b])
                outer_ref[rows, cols] = jnp.where(even, bottom[b], top[b])


def prepare_kernel(step_ref, jac_ref, scale_ref, half_ref):
    scale_ref[...] = 0.5 * step_ref[...]
    for d in range(3):
        for v in range(5):
            for w in range(5):
                row = (d * 5 + v) * 5 + w
                half_ref[row : row + 1, :] = jnp.full((1, 128), 0.5 * jac_ref[d, v, w], F32)


def weighted(half_ref, d, v, w, values):
    row = (d * 5 + v) * 5 + w
    line = half_ref[row : row + 1, :]
    return jnp.concatenate([line] * (values.shape[1] // 128), axis=1) * values


def section_kernel(got_ref, scale_ref, half_ref, part_ref, flow_ref):
    for v in range(5):
        for p in range(2):
            for m in range(2):
                row = p * 10 + m * 5 + v
                parts = [got_ref[pl.ds(a * ROWS + row, 16, 4 * ROWS), :] for a in range(4)]
                for s, halves_of in zip(LAYERS[m], paired(parts)):
                    base = (v * 4 + s) * 32 + p * 16
                    for b in range(2):
                        flow_ref[base : base + 16, 128 * b : 128 * b + 128] = halves_of[b]
    row = lax.broadcasted_iota(jnp.int32, (8, 256), 0)
    lane = lax.broadcasted_iota(jnp.int32, (8, 256), 1)
    at_top, at_bottom = row == 0, row == 7
    at_left, at_right = lane == 0, lane == 255
    for s in range(4):
        for t in range(4):
            diffs, smooth = [], []
            for v in range(5):
                base = (v * 4 + s) * 32 + t * 8
                here = flow_ref[base : base + 8, :]
                s_minus = flow_ref[base - 32 : base - 24, :] if s else jnp.zeros_like(here)
                s_plus = flow_ref[base + 32 : base + 40, :] if s < 3 else jnp.zeros_like(here)
                above = flow_ref[base - 1 : base, :] if t else 0.0
                below = flow_ref[base + 8 : base + 9, :] if t < 3 else 0.0
                p_minus = jnp.where(at_top, above, pltpu.roll(here, 1, 0))
                p_plus = jnp.where(at_bottom, below, pltpu.roll(here, 7, 0))
                a_minus = jnp.where(at_left, 0.0, pltpu.roll(here, 1, 1))
                a_plus = jnp.where(at_right, 0.0, pltpu.roll(here, 255, 1))
                diffs.append((s_plus - s_minus, p_plus - p_minus, a_plus - a_minus))
                total = (s_plus + s_minus) + (p_plus + p_minus) + (a_plus + a_minus)
                smooth.append((here, 0.75 * here - 0.125 * total))
            scale = scale_ref[s * 32 + t * 8 : s * 32 + t * 8 + 8, :]
            for v in range(5):
                here, resid = smooth[v]
                for d in range(3):
                    for w in range(5):
                        resid = resid + weighted(half_ref, d, v, w, diffs[w][d])
                base = (v * 4 + s) * 32 + t * 8
                part_ref[base : base + 8, :] = here - scale * resid


def applied(half_ref, d, sign, rows):
    out = []
    for v in range(5):
        total = -0.125 * rows[v]
        for w in range(5):
            term = weighted(half_ref, d, v, w, rows[w])
            total = total + term if sign > 0 else total - term
        out.append(total)
    return out


def finish_kernel(part_ref, far_ref, outer_ref, near_ref, inner_ref, scale_ref, half_ref, out_hbm, new_ref, sem):
    even, circ_even = (lax.axis_index(axis) & 1 == 0 for axis in ("span", "circ"))
    near, far = near_ref[...], far_ref[...]
    for v in range(5):
        new_ref[v * 128 : v * 128 + 128, :] = part_ref[v * 128 : v * 128 + 128, :]
    for edge, sign, rim in ((0, -1, jnp.where(circ_even, far, near)), (31, 1, jnp.where(circ_even, near, far))):
        for b in range(2):
            cols = slice(128 * b, 128 * b + 128)
            terms = applied(half_ref, 1, sign, [rim[b * 20 + v * 4 : b * 20 + v * 4 + 4] for v in range(5)])
            for s in range(4):
                scale = scale_ref[s * 32 + edge : s * 32 + edge + 1, cols]
                for v in range(5):
                    at = (v * 4 + s) * 32 + edge
                    new_ref[at : at + 1, cols] = part_ref[at : at + 1, cols] - scale * terms[v][s : s + 1]
    copies = []
    for v in range(5):
        rows = slice(v * 128 + 32, v * 128 + 96)
        copies.append(pltpu.make_async_copy(new_ref.at[rows, :], out_hbm.at[rows, :], sem.at[v]))
        copies[-1].start()
    for i, s in enumerate((0, 3)):
        for t in range(4):
            rows = []
            for v in range(5):
                side = slice(v * 32 + t * 8, v * 32 + t * 8 + 8)
                inner, outer = inner_ref[side, :], outer_ref[side, :]
                rows.append(jnp.where(even, inner, outer) if s else jnp.where(even, outer, inner))
            terms = applied(half_ref, 0, 1 if s else -1, rows)
            scale = scale_ref[s * 32 + t * 8 : s * 32 + t * 8 + 8, :]
            for v in range(5):
                at = slice((v * 4 + s) * 32 + t * 8, (v * 4 + s) * 32 + t * 8 + 8)
                new_ref[at, :] = new_ref[at, :] - scale * terms[v]
        for v in range(5):
            rows = slice((v * 4 + s) * 32, (v * 4 + s) * 32 + 32)
            copies.append(pltpu.make_async_copy(new_ref.at[rows, :], out_hbm.at[rows, :], sem.at[5 + 5 * i + v]))
            copies[-1].start()
    for copy in copies:
        copy.wait()


def local(coefficients, local_step, jacobian, harmonic_numbers, nodal_diameter):
    shape = jax.ShapeDtypeStruct
    ring = lax.axis_size("circ")
    cells = coefficients.transpose(1, 2, 3, 0).reshape(1280, 65)
    params = pltpu.CompilerParams(vmem_limit_bytes=8 << 20)
    sent = pl.pallas_call(
        expand_kernel,
        out_shape=shape((64 * ROWS, 128), F32),
        in_specs=[HBM, HBM, SMEM],
        out_specs=VMEM,
        scratch_shapes=[
            pltpu.VMEM((1280, 65), F32),
            pltpu.VMEM((1, 32), jnp.int32),
            pltpu.SemaphoreType.DMA((2,)),
        ],
        name="expand",
    )(cells, harmonic_numbers.reshape(1, 32), nodal_diameter)
    pairs = [(i, i + 1) for i in range(0, ring, 2)]
    between = [(i, (i + 1) % ring) for i in range(1, ring, 2)]
    got = lax.all_to_all(sent.reshape(64, 5, 4, 128), "circ", 0, 0, tiled=True)
    got = got.reshape(64 * ROWS, 128)
    scale, half = pl.pallas_call(
        prepare_kernel,
        out_shape=[shape((128, 256), F32), shape((80, 128), F32)],
        in_specs=[VMEM, SMEM],
        out_specs=[VMEM, VMEM],
        name="prepare",
        compiler_params=params,
    )(local_step.reshape(128, 256), jacobian)
    sizes = [(40, 128), (160, 256), (40, 128), (160, 256)]
    far, outer, near, inner = pl.pallas_call(
        edges_kernel,
        out_shape=[shape(size, F32) for size in sizes],
        in_specs=[VMEM],
        out_specs=[VMEM] * 4,
        scratch_shapes=[pltpu.VMEM((40, 128), F32)] * 2,
        name="edges",
        compiler_params=params,
    )(got)
    far = lax.ppermute(far, "circ", between + [(j, i) for i, j in between])
    outer = lax.ppermute(outer, "span", [(1, 2), (2, 1)])
    near = lax.ppermute(near, "circ", pairs + [(j, i) for i, j in pairs])
    inner = lax.ppermute(inner, "span", [(0, 1), (1, 0), (2, 3), (3, 2)])
    part = pl.pallas_call(
        section_kernel,
        out_shape=shape((640, 256), F32),
        in_specs=[VMEM] * 3,
        out_specs=VMEM,
        scratch_shapes=[pltpu.VMEM((640, 256), F32)],
        name="section",
        compiler_params=params,
        cost_estimate=pl.CostEstimate(flops=20_000_000, bytes_accessed=1_500_000, transcendentals=0),
    )(got, scale, half)
    new = pl.pallas_call(
        finish_kernel,
        out_shape=shape((640, 256), F32),
        in_specs=[VMEM] * 7,
        out_specs=HBM,
        scratch_shapes=[pltpu.VMEM((640, 256), F32), pltpu.SemaphoreType.DMA((15,))],
        name="finish",
        compiler_params=params,
    )(part, far, outer, near, inner, scale, half)
    return new.reshape(5, 4, 32, 256)


def solution(mesh):
    in_specs = (P(None, None, "span", "circ"), P("span", "circ", None), P(), P(), P())
    out_specs = P(None, "span", "circ", None)
    return jax.shard_map(local, mesh=mesh, in_specs=in_specs, out_specs=out_specs, check_vma=False)
```
